768 devices in a mesh: gx: 192 (over x, z_hi, y, core), gz: 4 (over z_lo).
Axes of the slice: x: 4, y: 8, z: 12 (z_hi: 3, z_lo: 4; z = z_hi * 4 + z_lo), core: 2. Of those that a mesh axis runs over, the one named last changes fastest.
Arguments:
- positions: float32 [3, 384, 64, 128], P(None, 'gx', 'gz'), may hold values from 0 to 1
- velocities: float32 [3, 384, 64, 128], P(None, 'gx', 'gz'), may hold values from -6 to 6
- forces: float32 [3, 384, 64, 128], P(None, 'gx', 'gz'), may hold values from -18 to 18
- charge: float32 [384, 64, 128], P('gx', 'gz'), may hold values from -3 to 3
- atom_type: int32 [384, 64, 128], P('gx', 'gz'), may hold values from 0 to 15
- bin_count: int32 [384, 64], P('gx', 'gz'), may hold values from 64 to 128
- exclusions: int32 [384, 64, 2, 16], P('gx', 'gz'), may hold values from 0 to 63, as said below
- repulsion: float32 [16, 16], replicated, may hold values from 0.5 to 5
Outputs:
- positions_out: float32 [3, 384, 64, 128], P(None, 'gx', 'gz')
- velocities_out: float32 [3, 384, 64, 128], P(None, 'gx', 'gz')
- forces_out: float32 [3, 384, 64, 128], P(None, 'gx', 'gz')
The draws below stay inside these ranges and needn't reach their ends.
Inputs may be any that keep to these rules, and one draw needn't show every extreme that they name: `exclusions`: each listed pair names two different slots below 64 of its bin.
All inputs are finite; a program needn't handle non-finite values.
Results may differ from the reference program's by a relative error of at most 0.0003.
Values sent between devices are 32-bit elements; how exact they have to be, the bound alone decides.
No kernel may reach another device: no remote copies, remote signals or barrier semaphores. Data moves between devices by JAX's collectives and lax.ppermute only.
A program may use at most 32 MiB of HBM per device.

```python
import math
import jax
import jax.numpy as jnp
from jax import lax

SLOTS = 128
NTYPES = 16
EXC = 16
STEPS = 2
NBX = 384
NBZ = 64


def draw_exclusions(key, part):
    first_key, second_key = jax.random.split(jax.random.fold_in(key, 11))
    half_slots = SLOTS // 2
    first_slot = jax.random.randint(first_key, (NBX, NBZ, 1, EXC), 0, half_slots)
    slot_gap = jax.random.randint(second_key, (NBX, NBZ, 1, EXC), 1, half_slots)
    second_slot = (first_slot + slot_gap) % half_slots
    return jnp.concatenate([first_slot, second_slot], axis=2).astype(jnp.int32)


def with_ends(values, rng, low, largest):
    index_at = [jax.random.randint(jax.random.fold_in(rng, axis), (), 0, length) for axis, length in enumerate(values.shape)]
    widest = values.shape.index(max(values.shape))
    next_to = index_at[:widest] + [(index_at[widest] + 1) % values.shape[widest]] + index_at[widest + 1:]
    return values.at[tuple(index_at)].set(low).at[tuple(next_to)].set(largest)


def level_of(own_key, extent, cuts, smallest, largest):
    loudness, own = 1.0, jax.random.fold_in(own_key, 6)
    for position, blocks in cuts:
        steps = jnp.exp(jax.random.uniform(jax.random.fold_in(own, position), (blocks,), jnp.float32, smallest / len(cuts), largest / len(cuts)))
        loudness = loudness * jnp.repeat(steps, extent[position] // blocks).reshape([-1 if axis == position else 1 for axis in range(len(extent))])
    return loudness


def centred(key, extent, deviation, bound, pieces=(), kind=jnp.bfloat16):
    entries = deviation * jax.random.normal(key, extent, jnp.float32)
    if pieces:
        entries = entries * level_of(key, extent, pieces, -0.22, 0.18)
    return jnp.clip(entries, -bound, bound).astype(kind)


def setup_inputs(seed: int = 0) -> dict:
    key_of = jax.random.split(jax.random.key(seed), 9)
    positions = jnp.clip(1.0 * jax.random.uniform(key_of[0], (3, NBX, NBZ, SLOTS), jnp.float32) ** level_of(key_of[0], (3, NBX, NBZ, SLOTS), ((1, 192), (2, 4)), -0.2, 0.2), 0.0, 1.0)
    velocities = centred(key_of[1], (3, NBX, NBZ, SLOTS), 1.0, 6.0, ((1, 192), (2, 4)), jnp.float32)
    forces = centred(key_of[2], (3, NBX, NBZ, SLOTS), 3.0, 18.0, ((1, 192), (2, 4)), jnp.float32)
    charge = centred(key_of[3], (NBX, NBZ, SLOTS), 0.5, 3.0, ((0, 192), (1, 4)), jnp.float32)
    atom_type = with_ends(jax.random.randint(key_of[4], (NBX, NBZ, SLOTS), 0, NTYPES), jax.random.fold_in(key_of[4], 1), 0, NTYPES - 1).astype(jnp.int32)
    bin_count = with_ends(jax.random.randint(key_of[5], (NBX, NBZ), SLOTS // 2, SLOTS + 1), jax.random.fold_in(key_of[5], 1), SLOTS // 2, SLOTS).astype(jnp.int32)
    exclusions = draw_exclusions(jax.random.fold_in(key_of[8], 71), 0)
    repulsion = jnp.clip(jnp.exp(jax.random.uniform(key_of[7], (NTYPES, NTYPES), jnp.float32, math.log(0.5), math.log(5.0))), 0.5, 5.0)
    return {"positions": positions, "velocities": velocities, "forces": forces, "charge": charge, "atom_type": atom_type, "bin_count": bin_count, "exclusions": exclusions, "repulsion": repulsion}


time_step = 0.05
core_sq = 0.09

def pack_atoms(positions, charge, atom_type, bin_count):
    slot_ids = jnp.arange(positions.shape[-1], dtype=jnp.int32)
    is_live = slot_ids < bin_count[..., None]
    type_code = jnp.where(is_live, atom_type + 1, 0).astype(jnp.float32)
    live_charge = jnp.where(is_live, charge, 0.0).astype(jnp.float32)
    return jnp.concatenate([positions, live_charge[None], type_code[None]], axis=0)

def soft_table(own_code, partner_code, table_ext):
    levels = jnp.arange(table_ext.shape[0], dtype=jnp.float32)
    hot_own = (own_code[..., None] == levels).astype(jnp.float32)
    hot_other = (partner_code[..., None] == levels).astype(jnp.float32)
    by_rows = jnp.einsum('bik,kl->bil', hot_own, table_ext, precision=lax.Precision.HIGHEST)
    return jnp.einsum('bil,bjl->bij', by_rows, hot_other, precision=lax.Precision.HIGHEST)

def exclusion_keep(pair_list, slot_total):
    levels = jnp.arange(slot_total, dtype=jnp.int32)
    first_hot = (pair_list[:, 0, :, None] == levels).astype(jnp.float32)
    second_hot = (pair_list[:, 1, :, None] == levels).astype(jnp.float32)
    matches = jnp.einsum('bei,bej->bij', first_hot, second_hot, precision=lax.Precision.HIGHEST)
    matches = matches + jnp.swapaxes(matches, 1, 2)
    return (matches == 0.0).astype(jnp.float32)

def pair_terms(own_atoms, partner, shift_x, shift_z, table_ext, keep_mask):
    delta_x = own_atoms[0][:, :, None] - partner[0][:, None, :] - shift_x
    delta_y = own_atoms[1][:, :, None] - partner[1][:, None, :]
    delta_z = own_atoms[2][:, :, None] - partner[2][:, None, :] - shift_z
    dist_sq = delta_x * delta_x + delta_y * delta_y + delta_z * delta_z
    inside = jnp.maximum(1.0 - dist_sq, 0.0)
    inverse = lax.rsqrt(dist_sq + core_sq)
    coulomb = own_atoms[3][:, :, None] * partner[3][:, None, :] * inside * inside * inverse * inverse * inverse
    scalar = soft_table(own_atoms[4], partner[4], table_ext) * inside + coulomb
    if keep_mask is not None:
        scalar = scalar * keep_mask
    on_own = jnp.stack([lax.optimization_barrier(jnp.sum(scalar * delta_x, axis=2)), lax.optimization_barrier(jnp.sum(scalar * delta_y, axis=2)), lax.optimization_barrier(jnp.sum(scalar * delta_z, axis=2))])
    on_partner = -jnp.stack([lax.optimization_barrier(jnp.sum(scalar * delta_x, axis=1)), lax.optimization_barrier(jnp.sum(scalar * delta_y, axis=1)), lax.optimization_barrier(jnp.sum(scalar * delta_z, axis=1))])
    return (on_own, on_partner)

def all_forces(packed, exclusions, table_ext):
    zero_row = jnp.zeros_like(packed[:, :, :1])
    upward = jnp.concatenate([packed[:, :, 1:], zero_row], axis=2)
    downward = jnp.concatenate([zero_row, packed[:, :, :-1]], axis=2)
    row_data = (packed, upward, jnp.roll(packed, -1, axis=1), jnp.roll(upward, -1, axis=1), jnp.roll(downward, -1, axis=1))
    row_data = tuple((jnp.moveaxis(member, 1, 0) for member in row_data)) + (exclusions,)

    def row_forces(inputs):
        current, current_up, ahead_row, ahead_up, ahead_down, pair_list = inputs
        keep_mask = exclusion_keep(pair_list, current.shape[-1])
        summed, unused = pair_terms(current, current, 0.0, 0.0, table_ext, keep_mask)
        on_own, lifted = pair_terms(current, current_up, 0.0, 1.0, table_ext, None)
        summed = summed + on_own
        blank_row = jnp.zeros_like(lifted[:, :1])
        summed = summed + jnp.concatenate([blank_row, lifted[:, :-1]], axis=1)
        on_own, lower = pair_terms(current, ahead_down, 1.0, -1.0, table_ext, None)
        summed = summed + on_own
        on_own, level = pair_terms(current, ahead_row, 1.0, 0.0, table_ext, None)
        summed = summed + on_own
        on_own, higher = pair_terms(current, ahead_up, 1.0, 1.0, table_ext, None)
        summed = summed + on_own
        ahead_forces = level + jnp.concatenate([lower[:, 1:], blank_row], axis=1) + jnp.concatenate([blank_row, higher[:, :-1]], axis=1)
        return (summed, ahead_forces)
    own_forces, ahead_forces = lax.map(row_forces, row_data)
    combined = own_forces + jnp.roll(ahead_forces, 1, axis=0)
    return jnp.moveaxis(combined, 0, 1)

def reference(positions, velocities, forces, charge, atom_type, bin_count, exclusions, repulsion):
    table_ext = jnp.pad(0.5 * (repulsion + repulsion.T), ((1, 0), (1, 0)))
    for step_number in range(STEPS):
        velocities = velocities + 0.5 * time_step * forces
        positions = positions + time_step * velocities
        packed = pack_atoms(positions, charge, atom_type, bin_count)
        forces = all_forces(packed, exclusions, table_ext)
        velocities = velocities + 0.5 * time_step * forces
    return (positions, velocities, forces)
```

```python
import functools

import jax
import jax.numpy as jnp
from jax import lax
from jax.experimental import pallas as pl
from jax.experimental.pallas import tpu as pltpu
from jax.sharding import PartitionSpec as P

DT = 0.05
CORE = 0.09
CHANNELS = 6
ROWS = 24
COLS = 4
BINS = ROWS * COLS
GROUPS = BINS // 8
RAW_A, RAW_B, RAW_W, RAW_Q = 0, 32, 96, 112
RAW = 120
BF = jnp.bfloat16
F32 = jnp.float32


def split3(value):
    high = value.astype(BF).astype(F32)
    rest = value - high
    mid = rest.astype(BF).astype(F32)
    return high, mid, rest - mid


def force_kernel(
    step, parity, own, near, far, vel, repulsion, *refs
):
    outs, (pos, raw, a_ref, b_ref, w_ref, acc, ut, qi, sh) = refs[:3], refs[3:]
    swap = parity[0] == 1
    zero = jnp.zeros((8, 128), F32)
    one = jnp.ones((8, 128), F32)

    def put(base, group, value):
        raw[pl.ds(group * 8 * RAW + base, 8, stride=RAW), :] = value

    per_col = ROWS // 8
    for group in range(GROUPS):
        col, inner = divmod(group, per_col)
        at = slice(inner * 8, inner * 8 + 8)
        if col in (1, 2):
            fields = [own[c, col - 1, at, :] for c in range(CHANNELS)]
        else:
            first, second = (far, near) if col == 0 else (near, far)
            fields = [jnp.where(swap, second[c, at, :], first[c, at, :]) for c in range(CHANNELS)]
        x, y, z, charge, code, names = fields
        x = x + (col - 1.5)
        for c, value in enumerate((x, y, z, charge, code)):
            pos[c, group * 8 : group * 8 + 8, :] = value
        for k, coord in enumerate((x, y, z)):
            h, m, l = split3(coord)
            base = RAW_A + (0, 6, 22)[k]
            for i, value in enumerate((h, h, m, h, l, m)):
                put(base + i, group, 2 * value)
            if k < 2:
                for i, value in enumerate((h, m, h, l, h, m)):
                    put(RAW_B + 6 * k + i, group, value)
            for i, value in enumerate((h, m, l)):
                put(RAW_W + 4 * i + k, group, value)
        flat = x * x + y * y
        for i, value in enumerate(split3(-(flat + z * z))):
            put(RAW_A + 16 + i, group, one)
            put(RAW_A + 19 + i, group, value)
        for v, shift in enumerate((-1.0, 0.0, 1.0)):
            other = z + shift
            base = RAW_B + 16 + 16 * v
            for i, value in enumerate(split3((1.0 - flat) - other * other)):
                put(base + i, group, value)
                put(base + 3 + i, group, one)
            h, m, l = split3(other)
            for i, value in enumerate((h, m, h, l, h, m)):
                put(base + 6 + i, group, value)
            for i in range(12, 16):
                put(base + i, group, zero)
        for i in range(12, 16):
            put(RAW_A + i, group, zero)
            put(RAW_A + 16 + i, group, zero)
            put(RAW_B + i, group, zero)
            put(RAW_W + i, group, zero)
        put(RAW_W + 3, group, one)
        put(RAW_W + 7, group, zero)
        put(RAW_W + 11, group, zero)
        for i, value in enumerate(split3(charge)):
            put(RAW_Q + i, group, value)
        put(RAW_Q + 3, group, names)
        for i in range(4, 8):
            put(RAW_Q + i, group, zero)

    code_rows = lax.broadcasted_iota(jnp.int32, (16, 128), 0).astype(F32) + 1.0
    table = 0.5 * (repulsion[...] + repulsion[...].T)
    table = jnp.concatenate(split3(table), axis=0).astype(BF)
    half_tile = jnp.zeros((8, 128), F32)

    def convert(b, carry):
        base = pl.multiple_of(b * RAW, 8)
        a_ref[b, 0:32, :] = raw[pl.ds(base + RAW_A, 32), :].astype(BF)
        b_ref[b, 0:64, :] = raw[pl.ds(base + RAW_B, 64), :].astype(BF)
        w_ref[b] = raw[pl.ds(base + RAW_W, 16), :].astype(BF)
        a_ref[b, 80:96, :] = jnp.concatenate([raw[pl.ds(base + RAW_Q, 8), :], half_tile], 0).astype(BF)
        hot = (pos[4, pl.ds(b, 1), :] == code_rows).astype(F32).astype(BF)
        b_ref[b, 64:80, :] = hot
        a_ref[b, 32:80, :] = jnp.dot(table, hot, preferred_element_type=F32).astype(BF)
        return carry

    lax.fori_loop(0, BINS, convert, 0, unroll=4)

    acc[...] = jnp.zeros_like(acc)
    row16 = lax.broadcasted_iota(jnp.int32, (16, 128), 0)
    spread = jnp.where(row16 < 3, 1.0, 0.0).astype(BF)
    spread_names = jnp.where(row16 == 3, 1.0, 0.0).astype(BF)
    slot = lax.broadcasted_iota(jnp.int32, (16, 128), 1).astype(F32)
    tilt = {0: None}
    for dz in (-1, 1):
        tilt[dz] = jnp.where(row16 == 12, float(dz), 0.0).astype(BF)
    zero_d = jnp.zeros((32, 128), BF)
    zero_t = jnp.zeros((48, 128), BF)

    def weights(b, dz):
        w = w_ref[b]
        if dz:
            w = w + tilt[dz]
        return jnp.concatenate([w, w], 1)

    def sweep(total, bin_of, pairs):
        ut[...] = jnp.zeros_like(ut)
        qi[...] = jnp.zeros_like(qi)
        sh[...] = jnp.zeros_like(sh)

        def reduce_stage(b):
            lhs, rhs = [], []
            for k, (offset, dz) in enumerate(pairs):
                both = sh[k]
                if offset and len(pairs) > 3:
                    lhs.append(weights(b + offset, dz))
                    rhs.append(both)
                stacked = jnp.concatenate([both[:, :128], both[:, 128:]], 0)
                acc[b + offset] += jnp.dot(weights(b, -dz), stacked, preferred_element_type=F32)
            if lhs:
                acc[b] += lax.dot_general(
                    jnp.concatenate(lhs, 1), jnp.concatenate(rhs, 1), (((1,), (1,)), ((), ())), preferred_element_type=F32
                )

        def scalar_stage(b):
            for k, (offset, dz) in enumerate(pairs):
                other = pos[3, pl.ds(b + offset, 1), :]
                for i in range(0, 128, 16):
                    reach = ut[k, i : i + 16, :128]
                    inside = jnp.maximum(reach, 0.0)
                    inverse = lax.rsqrt((1.0 + CORE) - reach)
                    coulomb = (qi[i : i + 16, :] * other) * inside * (inverse * inverse * inverse)
                    scalar = (ut[k, i : i + 16, 128:] + coulomb) * inside
                    high = scalar.astype(BF)
                    sh[k, i : i + 16, :128] = high
                    sh[k, i : i + 16, 128:] = (scalar - high.astype(F32)).astype(BF)

        def product_stage(b):
            a = a_ref[b].T
            for k, (offset, dz) in enumerate(pairs):
                other = b + offset
                b_dist = jnp.concatenate(
                    [b_ref[other, 0:16, :], b_ref[other, 32 + 16 * dz : 48 + 16 * dz, :]], axis=0
                )
                hot = b_ref[other, 64:80, :]
                left = [jnp.concatenate([b_dist, zero_t], 0)]
                right = jnp.concatenate([zero_d, hot, hot, hot], 0)
                lhs = a[:, 0:80]
                if not offset:
                    names = lax.dot_general(
                        a_ref[b, 80:96, :], spread_names, (((0,), (0,)), ((), ())), preferred_element_type=F32
                    )
                    first = (names[0:16, :] == slot).astype(F32)
                    second = (names[16:32, :] == slot).astype(F32)
                    drop = jnp.concatenate([first, second], 0)
                    again = jnp.concatenate([second, first], 0).astype(BF)
                    out = jnp.dot(lhs, jnp.concatenate([left[0], right], 1), preferred_element_type=F32)
                    hits = lax.dot_general(
                        drop.astype(BF), again, (((0,), (0,)), ((), ())), preferred_element_type=F32
                    )
                    ut[k, :, :128] = jnp.where(hits > 0.0, -1.0, out[:, :128])
                    ut[k, :, 128:] = out[:, 128:]
                else:
                    ut[k] = jnp.dot(lhs, jnp.concatenate([left[0], right], 1), preferred_element_type=F32)
            qi[...] = jnp.dot(a[:, 80:96], spread, preferred_element_type=F32)

        def body(n, carry):
            reduce_stage(bin_of(jnp.maximum(n - 2, 0)))
            scalar_stage(bin_of(jnp.clip(n - 1, 0, total - 1)))
            product_stage(bin_of(jnp.minimum(n, total - 1)))
            return carry

        lax.fori_loop(0, total + 2, body, 0)

    ahead = tuple((ROWS + dz, dz) for dz in (-1, 0, 1))
    sweep(18, lambda n: n + 1, ahead)
    sweep(36, lambda n: ROWS + 1 + n + (n // 18) * (ROWS - 18), ((0, 0), (1, 1)) + ahead)

    acc_flat = acc.reshape(BINS * 16, 128)
    for group in range(per_col, 3 * per_col):
        col, inner = divmod(group, per_col)
        at = slice(inner * 8, inner * 8 + 8)

        def take(k):
            return acc_flat[pl.ds(group * 128 + k, 8, stride=16), :]

        count = take(3)
        for c in range(3):
            here = pos[c, group * 8 : group * 8 + 8, :]
            back = (take(c) + take(4 + c)) + take(8 + c)
            if c == 2:
                back = back + take(12)
            force = here * count - back
            v = vel[c, col - 1, at, :] + 0.5 * DT * force
            if step == 0:
                v = v + 0.5 * DT * force
                outs[0][c, col - 1, at, :] = own[c, col - 1, at, :] + DT * v
            else:
                outs[0][c, col - 1, at, :] = own[c, col - 1, at, :]
                outs[2][c, col - 1, at, :] = force
            outs[1][c, col - 1, at, :] = v
    if step == 0:
        outs[2][...] = jnp.zeros_like(outs[2])


def forces_call(step, parity, own, near, far, vel, repulsion):
    out = jax.ShapeDtypeStruct((3, 2, ROWS, 128), F32)
    vmem = pl.BlockSpec(memory_space=pltpu.VMEM)
    return pl.pallas_call(
        functools.partial(force_kernel, step),
        out_shape=(out, out, out),
        in_specs=[pl.BlockSpec(memory_space=pltpu.SMEM), vmem, vmem, vmem, vmem, vmem],
        out_specs=(vmem, vmem, vmem),
        scratch_shapes=[
            pltpu.VMEM((5, BINS, 128), F32),
            pltpu.VMEM((BINS * RAW, 128), F32),
            pltpu.VMEM((BINS, 96, 128), BF),
            pltpu.VMEM((BINS, 80, 128), BF),
            pltpu.VMEM((BINS, 16, 128), BF),
            pltpu.VMEM((BINS, 16, 128), F32),
            pltpu.VMEM((5, 128, 256), F32),
            pltpu.VMEM((128, 128), F32),
            pltpu.VMEM((5, 128, 256), BF),
        ],
        compiler_params=pltpu.CompilerParams(vmem_limit_bytes=56 * 1024 * 1024),
        name=f"forces{step}",
    )(parity, own, near, far, vel, repulsion)


def swap_pairs(value, odd):
    count = lax.axis_size("gx")
    start = 1 if odd else 0
    route = []
    for i in range(start, count + start, 2):
        a, b = i % count, (i + 1) % count
        route += [(a, b), (b, a)]
    return lax.ppermute(value, "gx", route)


def with_rows(block):
    count = lax.axis_size("gz")
    up = [(i, i + 1) for i in range(count - 1)]
    down = [(b, a) for a, b in up]
    low = lax.ppermute(block[:, :, 17:18], "gz", up)
    high = lax.ppermute(block[:, :, 2:3], "gz", down)
    row = lax.broadcasted_iota(jnp.int32, (1, 1, ROWS, 1), 2)
    return jnp.where(row == 1, low, jnp.where(row == 18, high, block))


def exchanged(block, parity):
    own = with_rows(block)
    far = swap_pairs(jnp.where(parity == 1, own[:, 1], own[:, 0]), True)
    near = swap_pairs(jnp.where(parity == 1, own[:, 0], own[:, 1]), False)
    return own, near, far


def local(positions, velocities, forces, charge, atom_type, bin_count, exclusions, repulsion):
    columns, depth, slots = positions.shape[1:]
    velocities = velocities + 0.5 * DT * forces
    positions = positions + DT * velocities
    slot_ids = jnp.arange(slots, dtype=jnp.int32)
    live = slot_ids < bin_count[..., None]
    code = jnp.where(live, atom_type + 1, 0).astype(F32)
    live_charge = jnp.where(live, charge, 0.0)
    names = exclusions.reshape(columns, depth, -1).astype(F32)
    names = jnp.pad(names, ((0, 0), (0, 0), (0, slots - names.shape[-1])))
    packed = jnp.concatenate([positions, live_charge[None], code[None], names[None]], axis=0)
    place = ((0, 0), (0, 0), (2, ROWS - 2 - depth), (0, 0))
    packed = jnp.pad(packed, place)
    half = jnp.pad(velocities, place)
    parity = lax.axis_index("gx") % 2
    flag = parity.astype(jnp.int32).reshape(1)
    own, near, far = exchanged(packed, parity)
    p, v, _ = forces_call(0, flag, own, near, far, half, repulsion)
    p, near_p, far_p = exchanged(p, parity)
    own = jnp.concatenate([p, own[3:]], 0)
    near = jnp.concatenate([near_p, near[3:]], 0)
    far = jnp.concatenate([far_p, far[3:]], 0)
    outs = forces_call(1, flag, own, near, far, v, repulsion)
    return tuple(o[:, :, 2 : 2 + depth] for o in outs)


def solution(mesh):
    grid = P(None, "gx", "gz", None)
    return jax.shard_map(
        local,
        mesh=mesh,
        in_specs=(
            grid, grid, grid,
            P("gx", "gz", None), P("gx", "gz", None), P("gx", "gz"), P("gx", "gz", None, None), P(),
        ),
        out_specs=(grid, grid, grid),
        check_vma=False,
    )
```

```python
import functools

import jax
import jax.numpy as jnp
from jax import lax
from jax.experimental import pallas as pl
from jax.experimental.pallas import tpu as pltpu
from jax.sharding import PartitionSpec as P

DT = 0.05
CORE = 0.09
CHANNELS = 6
DEPTH = 16
ROWS = 24
USED = DEPTH + 2
RAW_A, RAW_W, RAW_Q, RAW_B = 0, 32, 48, 56
RAW = 120
BINS = 2 * ROWS
BF = jnp.bfloat16
F32 = jnp.float32


def split3(value):
    high = value.astype(BF).astype(F32)
    rest = value - high
    mid = rest.astype(BF).astype(F32)
    return high, mid, rest - mid


def raw_features(raw, group, fields, targets):
    x, y, z, charge, names = fields
    zero = jnp.zeros((8, 128), F32)
    one = jnp.ones((8, 128), F32)

    def put(base, value):
        raw[pl.ds(group * 8 * RAW + base, 8, stride=RAW), :] = value

    for k, coord in enumerate((x, y, z)):
        h, m, l = split3(coord)
        base = RAW_A + (0, 6, 22)[k]
        for i, value in enumerate((h, h, m, h, l, m)):
            put(base + i, 2 * value)
        if targets and k < 2:
            for i, value in enumerate((h, m, h, l, h, m)):
                put(RAW_B + 6 * k + i, value)
        for i, value in enumerate((h, m, l)):
            put(RAW_W + 4 * i + k, value)
    flat = x * x + y * y
    for i, value in enumerate(split3(-(flat + z * z))):
        put(RAW_A + 16 + i, one)
        put(RAW_A + 19 + i, value)
    put(RAW_W + 3, one)
    put(RAW_W + 7, zero)
    put(RAW_W + 11, zero)
    for i in range(12, 16):
        put(RAW_A + i, zero)
        put(RAW_A + 16 + i, zero)
        put(RAW_W + i, zero)
    for i, value in enumerate(split3(charge)):
        put(RAW_Q + i, value)
    put(RAW_Q + 3, names)
    for i in range(4, 8):
        put(RAW_Q + i, zero)
    if not targets:
        return
    for v, shift in enumerate((-1.0, 0.0, 1.0)):
        other = z + shift
        base = RAW_B + 16 + 16 * v
        for i, value in enumerate(split3((1.0 - flat) - other * other)):
            put(base + i, value)
            put(base + 3 + i, one)
        h, m, l = split3(other)
        for i, value in enumerate((h, m, h, l, h, m)):
            put(base + 6 + i, value)
        for i in range(12, 16):
            put(base + i, zero)
            if v == 0:
                put(RAW_B + i, zero)


def pack_features(raw, code, repulsion, at_ref, w_ref, qi_ref, b_ref):
    code_rows = lax.broadcasted_iota(jnp.int32, (16, 128), 0).astype(F32) + 1.0
    row16 = lax.broadcasted_iota(jnp.int32, (16, 128), 0)
    spread = jnp.where(row16 < 3, 1.0, 0.0).astype(BF)
    table = 0.5 * (repulsion[...] + repulsion[...].T)
    table = jnp.concatenate(split3(table), axis=0).astype(BF)
    half_tile = jnp.zeros((8, 128), F32)

    def one_bin(n, carry):
        b = (n // USED) * ROWS + n % USED
        base = pl.multiple_of(b * RAW, 8)
        hot = (code[pl.ds(b, 1), :] == code_rows).astype(F32).astype(BF)
        lookup = jnp.dot(table, hot, preferred_element_type=F32).astype(BF)
        tail = jnp.concatenate([raw[pl.ds(base + RAW_Q, 8), :], half_tile], 0).astype(BF)
        rows = jnp.concatenate([raw[pl.ds(base + RAW_A, 32), :].astype(BF), lookup, tail], 0)
        at_ref[b] = rows.T
        w_ref[b] = raw[pl.ds(base + RAW_W, 16), :].astype(BF)
        qi_ref[b] = lax.dot_general(tail, spread, (((0,), (0,)), ((), ())), preferred_element_type=F32)
        if b_ref is not None:
            b_ref[b, 0:64, :] = raw[pl.ds(base + RAW_B, 64), :].astype(BF)
            b_ref[b, 64:80, :] = hot
        return carry

    lax.fori_loop(0, 2 * USED, one_bin, 0, unroll=6)


def place_of(row):
    return jnp.where(row < 0, DEPTH, jnp.where(row >= DEPTH, DEPTH + 1, row))


def tilts():
    row16 = lax.broadcasted_iota(jnp.int32, (16, 128), 0)
    return {dz: jnp.where(row16 == 12, float(-dz), 0.0).astype(BF) for dz in (-1, 1)}


def scalar_block(reach, soft, charges):
    inside = jnp.maximum(reach, 0.0)
    inverse = lax.rsqrt((1.0 + CORE) - reach)
    coulomb = charges * inside * (inverse * inverse * inverse)
    scalar = (soft + coulomb) * inside
    high = scalar.astype(BF)
    return high, (scalar - high.astype(F32)).astype(BF)


def pipelined(product, scalar, reduce, buffers):
    for ref in buffers:
        ref[...] = jnp.zeros_like(ref)

    def body(n, carry):
        for half in (0, 1):
            step = 2 * n + half
            reduce(jnp.maximum(step - 2, 0), half)
            product(jnp.minimum(step, DEPTH - 1), half)
            scalar(jnp.clip(step - 1, 0, DEPTH - 1), 1 - half)
        return carry

    lax.fori_loop(0, DEPTH // 2 + 1, body, 0)


def inner_kernel(own, repulsion, acc, b_ref, raw, at_ref, w_ref, qi_ref, ut, sh):
    for group in range(6):
        col, inner = divmod(group, 3)
        at = slice(inner * 8, inner * 8 + 8)
        fields = [own[c, col, at, :] for c in (0, 1, 2, 3, 5)]
        fields[0] = fields[0] + (col - 0.5)
        raw_features(raw, group, fields, inner < 2)
    code = own.at[4].reshape(BINS, 128)
    charge = own.at[3].reshape(BINS, 128)
    pack_features(raw, code, repulsion, at_ref, w_ref, qi_ref, b_ref)
    tilt = tilts()
    row16 = lax.broadcasted_iota(jnp.int32, (16, 128), 0)
    spread_names = jnp.where(row16 == 3, 1.0, 0.0).astype(BF)
    slot = lax.broadcasted_iota(jnp.int32, (16, 128), 1).astype(F32)
    pairs = [(col, dz) for dz in (-1, 0, 1) for col in (0, 1)]

    def source(row, col, dz):
        return col * ROWS + place_of(row - dz)

    def product(row, slot_id):
        for k, (col, dz) in enumerate(pairs):
            b = source(row, col, dz)
            lhs = at_ref[b]
            sides = [
                jnp.concatenate(
                    [b_ref[t * ROWS + row, 0:16, :], b_ref[t * ROWS + row, 32 + 16 * dz : 48 + 16 * dz, :]], 0
                )
                for t in (0, 1)
            ]
            reach = jnp.dot(lhs[:, 0:32], jnp.concatenate(sides, 1), preferred_element_type=F32)
            hots = jnp.concatenate([b_ref[t * ROWS + row, 64:80, :] for t in (0, 1)], 1)
            soft = jnp.dot(lhs[:, 32:80], jnp.concatenate([hots] * 3, 0), preferred_element_type=F32)
            if dz == 0:
                listed = lax.dot_general(
                    own_names(b), spread_names, (((0,), (0,)), ((), ())), preferred_element_type=F32
                )
                first = (listed[0:16, :] == slot).astype(F32)
                second = (listed[16:32, :] == slot).astype(F32)
                hits = lax.dot_general(
                    jnp.concatenate([first, second], 0).astype(BF),
                    jnp.concatenate([second, first], 0).astype(BF),
                    (((0,), (0,)), ((), ())),
                    preferred_element_type=F32,
                )
                here = slice(128 * col, 128 * col + 128)
                there = slice(128 * (1 - col), 128 * (1 - col) + 128)
                ut[slot_id, k, :, here] = jnp.where(hits > 0.0, -1.0, reach[:, here])
                ut[slot_id, k, :, there] = reach[:, there]
            else:
                ut[slot_id, k, :, 0:256] = reach
            ut[slot_id, k, :, 256:512] = soft

    def own_names(b):
        base = pl.multiple_of(b * RAW, 8)
        tail = raw[pl.ds(base + RAW_Q, 8), :]
        return jnp.concatenate([tail, jnp.zeros((8, 128), F32)], 0).astype(BF)

    def scalar(row, slot_id):
        others = [charge[pl.ds(t * ROWS + row, 1), :] for t in (0, 1)]
        for k, (col, dz) in enumerate(pairs):
            b = source(row, col, dz)
            for i in range(0, 128, 16):
                mine = qi_ref[b, i : i + 16, :]
                for t in (0, 1):
                    lanes = slice(128 * t, 128 * t + 128)
                    high, low = scalar_block(
                        ut[slot_id, k, i : i + 16, lanes],
                        ut[slot_id, k, i : i + 16, 256 + 128 * t : 384 + 128 * t],
                        mine * others[t],
                    )
                    sh[slot_id, 0, 128 * k + i : 128 * k + i + 16, lanes] = high
                    sh[slot_id, 1, 128 * k + i : 128 * k + i + 16, lanes] = low

    def reduce(row, slot_id):
        parts = []
        for col, dz in pairs:
            w = w_ref[source(row, col, dz)]
            parts.append(w + tilt[dz] if dz else w)
        w = jnp.concatenate(parts, 1)
        total = jnp.dot(w, sh[slot_id, 0], preferred_element_type=F32)
        total = total + jnp.dot(w, sh[slot_id, 1], preferred_element_type=F32)
        acc[row] = total[:, :128]
        acc[DEPTH + row] = total[:, 128:]

    pipelined(product, scalar, reduce, (ut, sh))


def outer_kernel(
    step, parity, own, near, far, acc_in, b_ref, vel, repulsion, pos_out, vel_out, frc_out,
    raw, at_ref, w_ref, qi_ref, ut, sh, acc, code,
):
    swap = parity[0] == 1
    for group in range(6):
        side, inner = divmod(group, 3)
        at = slice(inner * 8, inner * 8 + 8)
        first, second = (far, near) if side == 0 else (near, far)
        fields = [jnp.where(swap, second[c, at, :], first[c, at, :]) for c in (0, 1, 2, 3, 4)]
        code[group * 8 : group * 8 + 8, :] = fields.pop()
        fields[0] = fields[0] + (-1.5, 1.5)[side]
        raw_features(raw, group, fields + [jnp.zeros((8, 128), F32)], False)
    pack_features(raw, code, repulsion, at_ref, w_ref, qi_ref, None)
    charge = own.at[3].reshape(BINS, 128)
    tilt = tilts()
    pairs = [(col, dz) for col in (0, 1) for dz in (-1, 0, 1)]
    zero_d = jnp.zeros((32, 128), BF)
    zero_t = jnp.zeros((48, 128), BF)

    def source(row, col, dz):
        return col * ROWS + place_of(row - dz)

    def product(row, slot_id):
        for k, (col, dz) in enumerate(pairs):
            lhs = at_ref[source(row, col, dz)][:, 0:80]
            target = col * ROWS + row
            hot = b_ref[target, 64:80, :]
            left = jnp.concatenate(
                [b_ref[target, 0:16, :], b_ref[target, 32 + 16 * dz : 48 + 16 * dz, :], zero_t], 0
            )
            right = jnp.concatenate([zero_d, hot, hot, hot], 0)
            ut[slot_id, k] = jnp.dot(lhs, jnp.concatenate([left, right], 1), preferred_element_type=F32)

    def scalar(row, slot_id):
        others = [charge[pl.ds(t * ROWS + row, 1), :] for t in (0, 1)]
        for k, (col, dz) in enumerate(pairs):
            b = source(row, col, dz)
            for i in range(0, 128, 16):
                high, low = scalar_block(
                    ut[slot_id, k, i : i + 16, 0:128],
                    ut[slot_id, k, i : i + 16, 128:256],
                    qi_ref[b, i : i + 16, :] * others[col],
                )
                at = 128 * (k % 3) + i
                sh[slot_id, col, at : at + 16, :] = high
                sh[slot_id, col, 384 + at : 400 + at, :] = low

    def reduce(row, slot_id):
        for side in (0, 1):
            parts = []
            for col, dz in pairs:
                if col == side:
                    w = w_ref[source(row, col, dz)]
                    parts.append(w + tilt[dz] if dz else w)
            w = jnp.concatenate(parts + parts, 1)
            acc[side * DEPTH + row] = acc_in[side * DEPTH + row] + jnp.dot(
                w, sh[slot_id, side], preferred_element_type=F32
            )

    pipelined(product, scalar, reduce, (ut, sh))

    flat = acc.reshape(2 * DEPTH * 16, 128)
    for group in range(4):
        col, inner = divmod(group, 2)
        at = slice(inner * 8, inner * 8 + 8)

        def take(k):
            return flat[pl.ds(group * 128 + k, 8, stride=16), :]

        count = take(3)
        for c in range(3):
            here = own[c, col, at, :]
            back = (take(c) + take(4 + c)) + take(8 + c)
            if c == 2:
                back = back + take(12)
            frame = here + (col - 0.5) if c == 0 else here
            force = frame * count - back
            v = vel[c, col, at, :] + 0.5 * DT * force
            if step == 0:
                v = v + 0.5 * DT * force
                here = here + DT * v
            pos_out[c, col, at, :] = here
            vel_out[c, col, at, :] = v
            frc_out[c, col, at, :] = force


VMEM = pl.BlockSpec(memory_space=pltpu.VMEM)
FEATURES = [
    pltpu.VMEM((BINS * RAW, 128), F32),
    pltpu.VMEM((BINS, 128, 96), BF),
    pltpu.VMEM((BINS, 16, 128), BF),
    pltpu.VMEM((BINS, 128, 128), F32),
]
LIMIT = pltpu.CompilerParams(vmem_limit_bytes=40 * 1024 * 1024)


def inner_call(step, own, repulsion):
    return pl.pallas_call(
        inner_kernel,
        out_shape=(
            jax.ShapeDtypeStruct((2 * DEPTH, 16, 128), F32),
            jax.ShapeDtypeStruct((BINS, 80, 128), BF),
        ),
        in_specs=[VMEM, VMEM],
        out_specs=(VMEM, VMEM),
        scratch_shapes=FEATURES
        + [pltpu.VMEM((2, 6, 128, 512), F32), pltpu.VMEM((2, 2, 768, 256), BF)],
        compiler_params=LIMIT,
        name=f"inner{step}",
    )(own, repulsion)


def outer_call(step, parity, own, near, far, acc, features, vel, repulsion):
    out = jax.ShapeDtypeStruct((3, 2, DEPTH, 128), F32)
    return pl.pallas_call(
        functools.partial(outer_kernel, step),
        out_shape=(out, out, out),
        in_specs=[pl.BlockSpec(memory_space=pltpu.SMEM)] + [VMEM] * 7,
        out_specs=(VMEM, VMEM, VMEM),
        scratch_shapes=FEATURES
        + [
            pltpu.VMEM((2, 6, 128, 256), F32),
            pltpu.VMEM((2, 2, 768, 128), BF),
            pltpu.VMEM((2 * DEPTH, 16, 128), F32),
            pltpu.VMEM((BINS, 128), F32),
        ],
        compiler_params=LIMIT,
        name=f"outer{step}",
    )(parity, own, near, far, acc, features, vel, repulsion)


def swap_pairs(value, odd):
    count = lax.axis_size("gx")
    start = 1 if odd else 0
    route = []
    for i in range(start, count + start, 2):
        a, b = i % count, (i + 1) % count
        route += [(a, b), (b, a)]
    return lax.ppermute(value, "gx", route)


def with_rows(block):
    count = lax.axis_size("gz")
    up = [(i, i + 1) for i in range(count - 1)]
    down = [(b, a) for a, b in up]
    low = lax.ppermute(block[:, :, DEPTH - 1 :], "gz", up)
    high = lax.ppermute(block[:, :, :1], "gz", down)
    pad = jnp.zeros(block.shape[:2] + (ROWS - USED, block.shape[3]), F32)
    return jnp.concatenate([block, low, high, pad], 2)


def exchanged(block, parity):
    own = with_rows(block)
    far = swap_pairs(jnp.where(parity == 1, own[:, 1], own[:, 0]), True)
    near = swap_pairs(jnp.where(parity == 1, own[:, 0], own[:, 1]), False)
    return own, near, far


def local(positions, velocities, forces, charge, atom_type, bin_count, exclusions, repulsion):
    columns, depth, slots = positions.shape[1:]
    velocities = velocities + 0.5 * DT * forces
    positions = positions + DT * velocities
    slot_ids = jnp.arange(slots, dtype=jnp.int32)
    live = slot_ids < bin_count[..., None]
    code = jnp.where(live, atom_type + 1, 0).astype(F32)
    live_charge = jnp.where(live, charge, 0.0)
    names = exclusions.reshape(columns, depth, -1).astype(F32)
    names = jnp.pad(names, ((0, 0), (0, 0), (0, slots - names.shape[-1])))
    packed = jnp.concatenate([positions, live_charge[None], code[None], names[None]], axis=0)
    parity = lax.axis_index("gx") % 2
    flag = parity.astype(jnp.int32).reshape(1)
    own, near, far = exchanged(packed, parity)
    acc, features = inner_call(0, own, repulsion)
    p, v, _ = outer_call(0, flag, own, near, far, acc, features, velocities, repulsion)
    p, near_p, far_p = exchanged(p, parity)
    own = jnp.concatenate([p, own[3:]], 0)
    near = jnp.concatenate([near_p, near[3:]], 0)
    far = jnp.concatenate([far_p, far[3:]], 0)
    acc, features = inner_call(1, own, repulsion)
    return outer_call(1, flag, own, near, far, acc, features, v, repulsion)


def solution(mesh):
    grid = P(None, "gx", "gz", None)
    return jax.shard_map(
        local,
        mesh=mesh,
        in_specs=(
            grid, grid, grid,
            P("gx", "gz", None), P("gx", "gz", None), P("gx", "gz"), P("gx", "gz", None, None), P(),
        ),
        out_specs=(grid, grid, grid),
        check_vma=False,
    )
```

```python
import functools

import jax
import jax.numpy as jnp
from jax import lax
from jax.experimental import pallas as pl
from jax.experimental.pallas import tpu as pltpu
from jax.sharding import PartitionSpec as P

DT = 0.05
CORE = 0.09
CHANNELS = 6
DEPTH = 16
ROWS = 24
USED = DEPTH + 2
RAW_A, RAW_W, RAW_Q, RAW_B = 0, 32, 48, 56
RAW = 120
BINS = 2 * ROWS
SLOTS = 3
BF = jnp.bfloat16
F32 = jnp.float32


def split3(value):
    high = value.astype(BF).astype(F32)
    rest = value - high
    mid = rest.astype(BF).astype(F32)
    return high, mid, rest - mid


def raw_features(raw, group, fields, targets):
    x, y, z, charge, names = fields
    zero = jnp.zeros((8, 128), F32)
    one = jnp.ones((8, 128), F32)

    def put(base, value):
        raw[pl.ds(group * 8 * RAW + base, 8, stride=RAW), :] = value

    for k, coord in enumerate((x, y, z)):
        h, m, l = split3(coord)
        base = RAW_A + (0, 6, 22)[k]
        for i, value in enumerate((h, h, m, h, l, m)):
            put(base + i, 2 * value)
        if targets and k < 2:
            for i, value in enumerate((h, m, h, l, h, m)):
                put(RAW_B + 6 * k + i, value)
        for i, value in enumerate((h, m, l)):
            put(RAW_W + 4 * i + k, value)
    flat = x * x + y * y
    for i, value in enumerate(split3(-(flat + z * z))):
        put(RAW_A + 16 + i, one)
        put(RAW_A + 19 + i, value)
    put(RAW_W + 3, one)
    put(RAW_W + 7, zero)
    put(RAW_W + 11, zero)
    for i in range(12, 16):
        put(RAW_A + i, zero)
        put(RAW_A + 16 + i, zero)
        put(RAW_W + i, zero)
    for i, value in enumerate(split3(charge)):
        put(RAW_Q + i, value)
    put(RAW_Q + 3, names)
    for i in range(4, 8):
        put(RAW_Q + i, zero)
    if not targets:
        return
    for v, shift in enumerate((-1.0, 0.0, 1.0)):
        other = z + shift
        base = RAW_B + 16 + 16 * v
        for i, value in enumerate(split3((1.0 - flat) - other * other)):
            put(base + i, value)
            put(base + 3 + i, one)
        h, m, l = split3(other)
        for i, value in enumerate((h, m, h, l, h, m)):
            put(base + 6 + i, value)
        for i in range(12, 16):
            put(base + i, zero)
            if v == 0:
                put(RAW_B + i, zero)


def pack_features(raw, code, repulsion, at_ref, w_ref, qi_ref, b_ref):
    code_rows = lax.broadcasted_iota(jnp.int32, (16, 128), 0).astype(F32) + 1.0
    row16 = lax.broadcasted_iota(jnp.int32, (16, 128), 0)
    spread = jnp.where(row16 < 3, 1.0, 0.0).astype(BF)
    table = 0.5 * (repulsion[...] + repulsion[...].T)
    table = jnp.concatenate(split3(table), axis=0).astype(BF)
    half_tile = jnp.zeros((8, 128), F32)

    def one_bin(n, carry):
        b = (n // USED) * ROWS + n % USED
        base = pl.multiple_of(b * RAW, 8)
        hot = (code[pl.ds(b, 1), :] == code_rows).astype(F32).astype(BF)
        lookup = jnp.dot(table, hot, preferred_element_type=F32).astype(BF)
        tail = jnp.concatenate([raw[pl.ds(base + RAW_Q, 8), :], half_tile], 0).astype(BF)
        rows = jnp.concatenate([raw[pl.ds(base + RAW_A, 32), :].astype(BF), lookup, tail], 0)
        at_ref[b] = rows.T
        w_ref[b] = raw[pl.ds(base + RAW_W, 16), :].astype(BF)
        qi_ref[b] = lax.dot_general(tail, spread, (((0,), (0,)), ((), ())), preferred_element_type=F32)
        if b_ref is not None:
            b_ref[b, 0:64, :] = raw[pl.ds(base + RAW_B, 64), :].astype(BF)
            b_ref[b, 64:80, :] = hot
        return carry

    lax.fori_loop(0, 2 * USED, one_bin, 0, unroll=6)


def place_of(row):
    return jnp.where(row < 0, DEPTH, jnp.where(row >= DEPTH, DEPTH + 1, row))


def tilts():
    row16 = lax.broadcasted_iota(jnp.int32, (16, 128), 0)
    return {dz: jnp.where(row16 == 12, float(-dz), 0.0).astype(BF) for dz in (-1, 1)}


def scalar_block(reach, soft, charges):
    inside = jnp.maximum(reach, 0.0)
    inverse = lax.rsqrt((1.0 + CORE) - reach)
    coulomb = charges * inside * (inverse * inverse * inverse)
    scalar = (soft + coulomb) * inside
    high = scalar.astype(BF)
    return high, (scalar - high.astype(F32)).astype(BF)


def pipelined(product, scalar, reduce):
    def body(n, carry):
        for part in range(SLOTS):
            step = SLOTS * n + part
            reduce(jnp.maximum(step - 2, 0), (part - 2) % SLOTS)
            product(jnp.minimum(step, DEPTH - 1), part)
            scalar(jnp.clip(step - 1, 0, DEPTH - 1), (part - 1) % SLOTS)
        return carry

    lax.fori_loop(0, (DEPTH + 2) // SLOTS, body, 0)


def inner_kernel(own, repulsion, acc, b_ref, raw, at_ref, w_ref, qi_ref, ut, sh):
    for group in range(6):
        col, inner = divmod(group, 3)
        at = slice(inner * 8, inner * 8 + 8)
        fields = [own[c, col, at, :] for c in (0, 1, 2, 3, 5)]
        fields[0] = fields[0] + (col - 0.5)
        raw_features(raw, group, fields, inner < 2)
    code = own.at[4].reshape(BINS, 128)
    charge = own.at[3].reshape(BINS, 128)
    pack_features(raw, code, repulsion, at_ref, w_ref, qi_ref, b_ref)
    tilt = tilts()
    row16 = lax.broadcasted_iota(jnp.int32, (16, 128), 0)
    spread_names = jnp.where(row16 == 3, 1.0, 0.0).astype(BF)
    slot = lax.broadcasted_iota(jnp.int32, (16, 128), 1).astype(F32)
    pairs = [(col, dz) for dz in (-1, 0, 1) for col in (0, 1)]

    def source(row, col, dz):
        return col * ROWS + place_of(row - dz)

    def product(row, slot_id):
        for k, (col, dz) in enumerate(pairs):
            b = source(row, col, dz)
            lhs = at_ref[b]
            sides = [
                jnp.concatenate(
                    [b_ref[t * ROWS + row, 0:16, :], b_ref[t * ROWS + row, 32 + 16 * dz : 48 + 16 * dz, :]], 0
                )
                for t in (0, 1)
            ]
            reach = jnp.dot(lhs[:, 0:32], jnp.concatenate(sides, 1), preferred_element_type=F32)
            hots = jnp.concatenate([b_ref[t * ROWS + row, 64:80, :] for t in (0, 1)], 1)
            soft = jnp.dot(lhs[:, 32:80], jnp.concatenate([hots] * 3, 0), preferred_element_type=F32)
            if dz == 0:
                listed = lax.dot_general(
                    own_names(b), spread_names, (((0,), (0,)), ((), ())), preferred_element_type=F32
                )
                first = (listed[0:16, :] == slot).astype(F32)
                second = (listed[16:32, :] == slot).astype(F32)
                hits = lax.dot_general(
                    jnp.concatenate([first, second], 0).astype(BF),
                    jnp.concatenate([second, first], 0).astype(BF),
                    (((0,), (0,)), ((), ())),
                    preferred_element_type=F32,
                )
                here = slice(128 * col, 128 * col + 128)
                there = slice(128 * (1 - col), 128 * (1 - col) + 128)
                ut[slot_id, k, :, here] = jnp.where(hits > 0.0, -1.0, reach[:, here])
                ut[slot_id, k, :, there] = reach[:, there]
            else:
                ut[slot_id, k, :, 0:256] = reach
            ut[slot_id, k, :, 256:512] = soft

    def own_names(b):
        base = pl.multiple_of(b * RAW, 8)
        tail = raw[pl.ds(base + RAW_Q, 8), :]
        return jnp.concatenate([tail, jnp.zeros((8, 128), F32)], 0).astype(BF)

    def scalar(row, slot_id):
        others = [charge[pl.ds(t * ROWS + row, 1), :] for t in (0, 1)]
        for k, (col, dz) in enumerate(pairs):
            b = source(row, col, dz)
            for i in range(0, 128, 16):
                mine = qi_ref[b, i : i + 16, :]
                for t in (0, 1):
                    lanes = slice(128 * t, 128 * t + 128)
                    high, low = scalar_block(
                        ut[slot_id, k, i : i + 16, lanes],
                        ut[slot_id, k, i : i + 16, 256 + 128 * t : 384 + 128 * t],
                        mine * others[t],
                    )
                    sh[slot_id, 0, 128 * k + i : 128 * k + i + 16, lanes] = high
                    sh[slot_id, 1, 128 * k + i : 128 * k + i + 16, lanes] = low

    def reduce(row, slot_id):
        parts = []
        for col, dz in pairs:
            w = w_ref[source(row, col, dz)]
            parts.append(w + tilt[dz] if dz else w)
        w = jnp.concatenate(parts, 1)
        total = jnp.dot(w, sh[slot_id, 0], preferred_element_type=F32)
        total = total + jnp.dot(w, sh[slot_id, 1], preferred_element_type=F32)
        acc[row] = total[:, :128]
        acc[DEPTH + row] = total[:, 128:]

    pipelined(product, scalar, reduce)


def outer_kernel(
    step, parity, own, near, far, acc_in, b_ref, vel, repulsion, pos_out, vel_out, frc_out,
    raw, at_ref, w_ref, qi_ref, ut, sh, acc, code,
):
    swap = parity[0] == 1
    for group in range(6):
        side, inner = divmod(group, 3)
        at = slice(inner * 8, inner * 8 + 8)
        first, second = (far, near) if side == 0 else (near, far)
        fields = [jnp.where(swap, second[c, at, :], first[c, at, :]) for c in (0, 1, 2, 3, 4)]
        code[group * 8 : group * 8 + 8, :] = fields.pop()
        fields[0] = fields[0] + (-1.5, 1.5)[side]
        raw_features(raw, group, fields + [jnp.zeros((8, 128), F32)], False)
    pack_features(raw, code, repulsion, at_ref, w_ref, qi_ref, None)
    charge = own.at[3].reshape(BINS, 128)
    tilt = tilts()
    pairs = [(col, dz) for col in (0, 1) for dz in (-1, 0, 1)]
    zero_d = jnp.zeros((32, 128), BF)
    zero_t = jnp.zeros((48, 128), BF)

    def source(row, col, dz):
        return col * ROWS + place_of(row - dz)

    def product(row, slot_id):
        for k, (col, dz) in enumerate(pairs):
            lhs = at_ref[source(row, col, dz)][:, 0:80]
            target = col * ROWS + row
            hot = b_ref[target, 64:80, :]
            left = jnp.concatenate(
                [b_ref[target, 0:16, :], b_ref[target, 32 + 16 * dz : 48 + 16 * dz, :], zero_t], 0
            )
            right = jnp.concatenate([zero_d, hot, hot, hot], 0)
            ut[slot_id, k] = jnp.dot(lhs, jnp.concatenate([left, right], 1), preferred_element_type=F32)

    def scalar(row, slot_id):
        others = [charge[pl.ds(t * ROWS + row, 1), :] for t in (0, 1)]
        for k, (col, dz) in enumerate(pairs):
            b = source(row, col, dz)
            for i in range(0, 128, 16):
                high, low = scalar_block(
                    ut[slot_id, k, i : i + 16, 0:128],
                    ut[slot_id, k, i : i + 16, 128:256],
                    qi_ref[b, i : i + 16, :] * others[col],
                )
                at = 128 * (k % 3) + i
                sh[slot_id, col, at : at + 16, :] = high
                sh[slot_id, col, 384 + at : 400 + at, :] = low

    def reduce(row, slot_id):
        for side in (0, 1):
            parts = []
            for col, dz in pairs:
                if col == side:
                    w = w_ref[source(row, col, dz)]
                    parts.append(w + tilt[dz] if dz else w)
            w = jnp.concatenate(parts + parts, 1)
            acc[side * DEPTH + row] = acc_in[side * DEPTH + row] + jnp.dot(
                w, sh[slot_id, side], preferred_element_type=F32
            )

    pipelined(product, scalar, reduce)

    flat = acc.reshape(2 * DEPTH * 16, 128)
    for group in range(4):
        col, inner = divmod(group, 2)
        at = slice(inner * 8, inner * 8 + 8)

        def take(k):
            return flat[pl.ds(group * 128 + k, 8, stride=16), :]

        count = take(3)
        for c in range(3):
            here = own[c, col, at, :]
            back = (take(c) + take(4 + c)) + take(8 + c)
            if c == 2:
                back = back + take(12)
            frame = here + (col - 0.5) if c == 0 else here
            force = frame * count - back
            v = vel[c, col, at, :] + 0.5 * DT * force
            if step == 0:
                v = v + 0.5 * DT * force
                here = here + DT * v
            pos_out[c, col, at, :] = here
            vel_out[c, col, at, :] = v
            frc_out[c, col, at, :] = force


VMEM = pl.BlockSpec(memory_space=pltpu.VMEM)
FEATURES = [
    pltpu.VMEM((BINS * RAW, 128), F32),
    pltpu.VMEM((BINS, 128, 96), BF),
    pltpu.VMEM((BINS, 16, 128), BF),
    pltpu.VMEM((BINS, 128, 128), F32),
]
LIMIT = pltpu.CompilerParams(vmem_limit_bytes=40 * 1024 * 1024)


def inner_call(step, own, repulsion):
    return pl.pallas_call(
        inner_kernel,
        out_shape=(
            jax.ShapeDtypeStruct((2 * DEPTH, 16, 128), F32),
            jax.ShapeDtypeStruct((BINS, 80, 128), BF),
        ),
        in_specs=[VMEM, VMEM],
        out_specs=(VMEM, VMEM),
        scratch_shapes=FEATURES
        + [pltpu.VMEM((SLOTS, 6, 128, 512), F32), pltpu.VMEM((SLOTS, 2, 768, 256), BF)],
        compiler_params=LIMIT,
        name=f"inner{step}",
    )(own, repulsion)


def outer_call(step, parity, own, near, far, acc, features, vel, repulsion):
    out = jax.ShapeDtypeStruct((3, 2, DEPTH, 128), F32)
    return pl.pallas_call(
        functools.partial(outer_kernel, step),
        out_shape=(out, out, out),
        in_specs=[pl.BlockSpec(memory_space=pltpu.SMEM)] + [VMEM] * 7,
        out_specs=(VMEM, VMEM, VMEM),
        scratch_shapes=FEATURES
        + [
            pltpu.VMEM((SLOTS, 6, 128, 256), F32),
            pltpu.VMEM((SLOTS, 2, 768, 128), BF),
            pltpu.VMEM((2 * DEPTH, 16, 128), F32),
            pltpu.VMEM((BINS, 128), F32),
        ],
        compiler_params=LIMIT,
        name=f"outer{step}",
    )(parity, own, near, far, acc, features, vel, repulsion)


def swap_pairs(value, odd):
    count = lax.axis_size("gx")
    start = 1 if odd else 0
    route = []
    for i in range(start, count + start, 2):
        a, b = i % count, (i + 1) % count
        route += [(a, b), (b, a)]
    return lax.ppermute(value, "gx", route)


def with_rows(block):
    count = lax.axis_size("gz")
    odd = lax.axis_index("gz") % 2 == 1
    top, bottom = block[:, :, DEPTH - 1 :], block[:, :, :1]

    def swapped(value, start):
        route = []
        for i in range(start, count - 1, 2):
            route += [(i, i + 1), (i + 1, i)]
        return lax.ppermute(value, "gz", route)

    first = swapped(jnp.where(odd, bottom, top), 0)
    second = swapped(jnp.where(odd, top, bottom), 1)
    low = jnp.where(odd, first, second)
    high = jnp.where(odd, second, first)
    pad = jnp.zeros(block.shape[:2] + (ROWS - USED, block.shape[3]), F32)
    return jnp.concatenate([block, low, high, pad], 2)


def exchanged(block, parity):
    own = with_rows(block)
    far = swap_pairs(jnp.where(parity == 1, own[:, 1], own[:, 0]), True)
    near = swap_pairs(jnp.where(parity == 1, own[:, 0], own[:, 1]), False)
    return own, near, far


def local(positions, velocities, forces, charge, atom_type, bin_count, exclusions, repulsion):
    columns, depth, slots = positions.shape[1:]
    velocities = velocities + 0.5 * DT * forces
    positions = positions + DT * velocities
    slot_ids = jnp.arange(slots, dtype=jnp.int32)
    live = slot_ids < bin_count[..., None]
    code = jnp.where(live, atom_type + 1, 0).astype(F32)
    live_charge = jnp.where(live, charge, 0.0)
    names = exclusions.reshape(columns, depth, -1).astype(F32)
    names = jnp.pad(names, ((0, 0), (0, 0), (0, slots - names.shape[-1])))
    packed = jnp.concatenate([positions, live_charge[None], code[None], names[None]], axis=0)
    parity = lax.axis_index("gx") % 2
    flag = parity.astype(jnp.int32).reshape(1)
    own, near, far = exchanged(packed, parity)
    acc, features = inner_call(0, own, repulsion)
    p, v, _ = outer_call(0, flag, own, near, far, acc, features, velocities, repulsion)
    p, near_p, far_p = exchanged(p, parity)
    own = jnp.concatenate([p, own[3:]], 0)
    near = jnp.concatenate([near_p, near[3:]], 0)
    far = jnp.concatenate([far_p, far[3:]], 0)
    acc, features = inner_call(1, own, repulsion)
    return outer_call(1, flag, own, near, far, acc, features, v, repulsion)


def solution(mesh):
    grid = P(None, "gx", "gz", None)
    return jax.shard_map(
        local,
        mesh=mesh,
        in_specs=(
            grid, grid, grid,
            P("gx", "gz", None), P("gx", "gz", None), P("gx", "gz"), P("gx", "gz", None, None), P(),
        ),
        out_specs=(grid, grid, grid),
        check_vma=False,
    )
```
